32 devices in a mesh: grp: 4 (over x, core), sec: 8 (over z, y).
Axes of the slice: x: 2, y: 2, z: 4, core: 2. Of those that a mesh axis runs over, the one named last changes fastest.
Arguments:
- trial: bfloat16 [2, 8, 256, 256], P(None, 'sec', 'grp'), may hold values from -6 to 6
- left_ops: bfloat16 [64, 8, 256, 256], P('grp', 'sec'), may hold values from -0.375 to 0.375
- right_ops: bfloat16 [64, 8, 256, 256], P('grp', 'sec'), may hold values from -0.046875 to 0.046875
- source: int32 [64, 8], P('grp', 'sec'), may hold values from 0 to 7
- live: int32 [64, 8], P('grp', 'sec'), may hold values 0 or 1
Outputs:
- sigma: bfloat16 [2, 8, 256, 256], P(None, 'sec', 'grp')
The draws below stay inside these ranges and needn't reach their ends.
All inputs are finite; a program needn't handle non-finite values. No bound on the sum of `live` on one device may be relied on, other than what follows from the above.
Results may differ from the reference program's by a relative error of at most 0.0049.
Values may be sent and summed in bfloat16 or wider, within the bound.
No kernel may reach another device: no remote copies, remote signals or barrier semaphores. Data moves between devices by JAX's collectives and lax.ppermute only.
A program may use at most 64 MiB of HBM per device.

```python
import jax
import jax.numpy as jnp
from jax import lax

BLK = 256
SECTORS = 8
OPS = 64


def touch_ends(result, stream_key, smallest, high):
    spot = [jax.random.randint(jax.random.fold_in(stream_key, axis), (), 0, length) for axis, length in enumerate(result.shape)]
    longest = result.shape.index(max(result.shape))
    next_to = spot[:longest] + [(spot[longest] + 1) % result.shape[longest]] + spot[longest + 1:]
    return result.at[tuple(spot)].set(smallest).at[tuple(next_to)].set(high)


def levels(stream_key, dims, pieces, low, top_value):
    gain, own = 1.0, jax.random.fold_in(stream_key, 6)
    for position, blocks in pieces:
        heights = jnp.exp(jax.random.uniform(jax.random.fold_in(own, position), (blocks,), jnp.float32, low / len(pieces), top_value / len(pieces)))
        gain = gain * jnp.repeat(heights, dims[position] // blocks).reshape([-1 if axis == position else 1 for axis in range(len(dims))])
    return gain


def centred(own_key, shape, deviation, bound, pieces=(), held_as=jnp.bfloat16):
    values = deviation * jax.random.normal(own_key, shape, jnp.float32)
    if pieces:
        values = values * levels(own_key, shape, pieces, -0.22, 0.18)
    return jnp.clip(values, -bound, bound).astype(held_as)


def setup_inputs(seed: int = 0) -> dict:
    streams_of = jax.random.split(jax.random.key(seed), 6)
    trial = centred(streams_of[0], (2, SECTORS, BLK, BLK), 1.0, 6.0, ((1, 8), (2, 4)))
    left_ops = centred(streams_of[1], (OPS, SECTORS, BLK, BLK), BLK ** -0.5, 0.375, ((0, 4), (1, 8)))
    right_ops = centred(streams_of[2], (OPS, SECTORS, BLK, BLK), (BLK * OPS) ** -0.5, 0.046875, ((0, 4), (1, 8)))
    source = touch_ends(jax.random.randint(streams_of[3], (OPS, SECTORS), 0, SECTORS), jax.random.fold_in(streams_of[3], 1), 0, SECTORS - 1).astype(jnp.int32)
    live = touch_ends((jax.random.randint(streams_of[4], (OPS, SECTORS), 0, 4) < 3).astype(jnp.int32), jax.random.fold_in(streams_of[4], 1), 0, 1)
    return dict(trial=trial, left_ops=left_ops, right_ops=right_ops, source=source, live=live)


def reference(trial, left_ops, right_ops, source, live):
    def one_sector(target):
        left = lax.dynamic_index_in_dim(left_ops, target, 1, keepdims=False)
        right = lax.dynamic_index_in_dim(right_ops, target, 1, keepdims=False)
        picks = lax.dynamic_index_in_dim(source, target, 1, keepdims=False).astype(jnp.int32)
        present = lax.dynamic_index_in_dim(live, target, 1, keepdims=False)
        picked = jnp.take(trial, picks, axis=1)
        inner = jnp.einsum("kab,vkbc->vkac", left.astype(jnp.float32), picked.astype(jnp.float32))
        inner = lax.optimization_barrier(inner.astype(jnp.bfloat16)).astype(jnp.float32)
        inner = inner * present.astype(jnp.float32)[None, :, None, None]
        return jnp.einsum("vkac,kdc->vad", inner, right.astype(jnp.float32))

    blocks = lax.map(one_sector, jnp.arange(SECTORS, dtype=jnp.int32))
    return jnp.transpose(blocks, (1, 0, 2, 3)).astype(jnp.bfloat16)
```

```python
import functools

import jax
import jax.numpy as jnp
from jax import lax
from jax.experimental import pallas as pl
from jax.experimental.pallas import tpu as pltpu
from jax.sharding import PartitionSpec as P


def hop(value, sizes, grp_mask, sec_mask):
    grp, sec = sizes
    pairs = [
        (g * sec + s, (g ^ grp_mask) * sec + (s ^ sec_mask)) for g in range(grp) for s in range(sec)
    ]
    return lax.ppermute(value, ("grp", "sec"), pairs)


def products(keys, ops, count, *refs):
    pick, live, place = ops
    pieces = refs[:count]
    left, right = refs[count], refs[count + 1]
    outs = refs[count + 2 : -4]
    table, total, loaded, arrival = refs[-4:]
    loads = [
        pltpu.make_async_copy(right.at[k], loaded.at[k], arrival.at[k]) for k in range(right.shape[0])
    ]
    for load in loads:
        load.start()
    for (piece_keys, ref) in zip(keys, pieces):
        rows = ref.shape[2]
        for n, (grp_mask, sec_rel) in enumerate(piece_keys):
            start = pl.multiple_of((place[0] ^ grp_mask) * rows, rows)
            for v in range(2):
                cols = ref.shape[3]
                table[sec_rel, pl.ds(start, rows), v * cols : (v + 1) * cols] = ref[n, v]
    size = left.shape[1]
    total[...] = jnp.zeros_like(total)
    for k in range(left.shape[0]):
        inner = jnp.dot(left[k], table[pick[k]], preferred_element_type=jnp.float32)
        inner = inner.astype(jnp.bfloat16) * live[k].astype(jnp.bfloat16)
        loads[k].wait()
        for v in range(2):
            total[v] += lax.dot_general(
                inner[:, v * size : (v + 1) * size],
                loaded[k],
                (((1,), (1,)), ((), ())),
                preferred_element_type=jnp.float32,
            )
    for grp_mask, out in enumerate(outs):
        rows = out.shape[1]
        start = pl.multiple_of((place[0] ^ grp_mask) * rows, rows)
        out[...] = total[:, pl.ds(start, rows), :].astype(out.dtype)


def kernel(keys, count, pick, live, place, *refs):
    products(keys, (pick, live, place), count, *refs)


def body(sizes, trial, left_ops, right_ops, source, live):
    grp, sec = sizes
    own = trial[:, 0]
    trials, rows, cols = own.shape
    lines = {0: own}
    for line in reversed(range(1, sec // 2)):
        lines[line] = hop(own, sizes, 0, 2 * line)
    planes = [(2 * g, y) for g in range(grp // 2) for y in range(2)]
    groups = []
    for line in range(sec // 2):
        group = [((0, 2 * line), lines[line])]
        for g, y in reversed(planes[1:]):
            group.append(((g, 2 * line + y), hop(lines[line], sizes, g, y)))
        groups.append(group)
    keys, pieces = [], []
    for group in groups:
        stacked = jnp.stack([value for _, value in group])
        keys.append([key for key, _ in group])
        pieces.append(stacked)
        keys.append([(g ^ 1, s) for (g, s), _ in group])
        pieces.append(hop(stacked, sizes, 1, 0))
    pick = source[:, 0] ^ lax.axis_index("sec").astype(jnp.int32)
    place = lax.axis_index("grp").astype(jnp.int32)[None]
    size = left_ops.shape[2]
    table = 2 * sec * trials * size * cols
    factor = 2 * left_ops.size
    vmem = pl.BlockSpec(memory_space=pltpu.VMEM)
    smem = pl.BlockSpec(memory_space=pltpu.SMEM)
    parts = pl.pallas_call(
        functools.partial(kernel, keys, len(pieces)),
        out_shape=[
            jax.ShapeDtypeStruct((trials, rows, cols), jnp.bfloat16 if g else jnp.float32)
            for g in range(grp)
        ],
        in_specs=[smem] * 3 + [vmem] * (len(pieces) + 1) + [pl.BlockSpec(memory_space=pl.ANY)],
        out_specs=[vmem] * grp,
        scratch_shapes=[
            pltpu.VMEM((sec, size, trials * cols), jnp.bfloat16),
            pltpu.VMEM((trials, size, cols), jnp.float32),
            pltpu.VMEM((right_ops.shape[0], size, cols), jnp.bfloat16),
            pltpu.SemaphoreType.DMA((right_ops.shape[0],)),
        ],
        compiler_params=pltpu.CompilerParams(vmem_limit_bytes=2 * table + 2 * factor + (6 << 20)),
    )(pick, live[:, 0], place, *pieces, left_ops[:, 0], right_ops[:, 0])
    mine = parts[0]
    arrived = [hop(parts[g], sizes, g, 0) for g in reversed(range(1, grp))]
    for value in arrived:
        mine = mine + value.astype(jnp.float32)
    return mine.astype(jnp.bfloat16)[:, None]


def solution(mesh):
    in_specs = (
        P(None, "sec", "grp", None),
        P("grp", "sec", None, None),
        P("grp", "sec", None, None),
        P("grp", "sec"),
        P("grp", "sec"),
    )
    out_specs = P(None, "sec", "grp", None)
    sizes = (mesh.shape["grp"], mesh.shape["sec"])
    return jax.shard_map(
        functools.partial(body, sizes), mesh=mesh, in_specs=in_specs, out_specs=out_specs, check_vma=False
    )
```
